32 devices in a mesh: dp: 8 (over y, x, core), seq: 4 (over z).
Axes of the slice: x: 2, y: 2, z: 4, core: 2. Of those that a mesh axis runs over, the one named last changes fastest.
Arguments:
- hidden_in: bfloat16 [24, 2048, 1024], P('dp', 'seq'), may hold values from -6 to 6
- cotangent: bfloat16 [24, 2048, 1024], P('dp', 'seq'), may hold values from -6 to 6
- first_gain: bfloat16 [1024], P(('dp', 'seq')), may hold values from 0.099609375 to 1.8984375
- first_shift: bfloat16 [1024], P(('dp', 'seq')), may hold values from -3 to 3
- triple_weight: bfloat16 [1024, 3072], P(('dp', 'seq')), may hold values from -0.1875 to 0.1875
- triple_bias: bfloat16 [3072], P(('dp', 'seq')), may hold values from -3 to 3
- dense_weight: bfloat16 [1024, 1024], P(('dp', 'seq')), may hold values from -0.75 to 0.75
- dense_bias: bfloat16 [1024], P(('dp', 'seq')), may hold values from -3 to 3
- second_gain: bfloat16 [1024], P(('dp', 'seq')), may hold values from 0.099609375 to 1.8984375
- second_shift: bfloat16 [1024], P(('dp', 'seq')), may hold values from -3 to 3
- expand_weight: bfloat16 [1024, 4096], P(('dp', 'seq')), may hold values from -0.1875 to 0.1875
- expand_bias: bfloat16 [4096], P(('dp', 'seq')), may hold values from -3 to 3
- contract_weight: bfloat16 [4096, 1024], P(('dp', 'seq')), may hold values from -0.09375 to 0.09375
- contract_bias: bfloat16 [1024], P(('dp', 'seq')), may hold values from -3 to 3
Outputs:
- block_out: bfloat16 [24, 2048, 1024], P('dp', 'seq')
- grad_input: float32 [24, 2048, 1024], P('dp', 'seq')
- grad_first_gain: float32 [1024], P(('dp', 'seq'))
- grad_first_shift: float32 [1024], P(('dp', 'seq'))
- grad_triple_weight: float32 [1024, 3072], P(('dp', 'seq'))
- grad_triple_bias: float32 [3072], P(('dp', 'seq'))
- grad_dense_weight: float32 [1024, 1024], P(('dp', 'seq'))
- grad_dense_bias: float32 [1024], P(('dp', 'seq'))
- grad_second_gain: float32 [1024], P(('dp', 'seq'))
- grad_second_shift: float32 [1024], P(('dp', 'seq'))
- grad_expand_weight: float32 [1024, 4096], P(('dp', 'seq'))
- grad_expand_bias: float32 [4096], P(('dp', 'seq'))
- grad_contract_weight: float32 [4096, 1024], P(('dp', 'seq'))
- grad_contract_bias: float32 [1024], P(('dp', 'seq'))
The draws below stay inside these ranges and needn't reach their ends.
All inputs are finite; a program needn't handle non-finite values.
Results may differ from the reference program's by a relative error of at most 0.0098.
Values may be sent and summed in bfloat16 or wider, within the bound.
A program may use at most 448 MiB of HBM per device.

```python
import math
import jax
import jax.numpy as jnp
from jax import lax

D = 1024
H = 16
HD = 64
FF = 4096
ROT = 16
LEN = 2048
SEQS = 24


def steps_of(own_key, shape, split, smallest, top_value):
    def one(axis_at, blocks):
        heights = jax.random.uniform(jax.random.fold_in(jax.random.fold_in(own_key, 6), axis_at), (blocks,), jnp.float32, smallest / len(split), top_value / len(split))
        return jnp.repeat(jnp.exp(heights), shape[axis_at] // blocks).reshape((-1,) + (1,) * (len(shape) - axis_at - 1))

    loudness = one(*split[0])
    for cut in split[1:]:
        loudness = loudness * one(*cut)
    return loudness


def bell_draw(key, extent, spread, most, cuts=(), held_as=jnp.bfloat16):
    values = spread * jax.random.normal(key, extent, jnp.float32)
    if cuts:
        values = values * steps_of(key, extent, cuts, -0.22, 0.18)
    return jnp.clip(values, -most, most).astype(held_as)


def setup_inputs(seed: int = 0) -> dict:
    streams_of = jax.random.split(jax.random.key(seed), 15)
    hidden_in = bell_draw(streams_of[0], (SEQS, LEN, D), 1.0, 6.0, ((0, 8), (1, 4)))
    cotangent = bell_draw(streams_of[1], (SEQS, LEN, D), 1.0, 6.0, ((0, 8), (1, 4)))
    first_gain = jnp.clip(1.0 + 0.18 * jax.random.normal(streams_of[2], (D,), jnp.float32), 0.099609375, 1.8984375).astype(jnp.bfloat16)
    first_shift = bell_draw(streams_of[3], (D,), 0.5, 3.0, ((0, 32),))
    triple_weight = bell_draw(streams_of[4], (D, 3 * D), D ** -0.5, 0.1875, ((0, 32),))
    triple_bias = bell_draw(streams_of[5], (3 * D,), 0.5, 3.0, ((0, 32),))
    dense_weight = bell_draw(streams_of[6], (D, D), (D // 16) ** -0.5, 0.75, ((0, 32),))
    dense_bias = bell_draw(streams_of[7], (D,), 0.5, 3.0, ((0, 32),))
    second_gain = jnp.clip(1.0 + 0.18 * jax.random.normal(streams_of[8], (D,), jnp.float32), 0.099609375, 1.8984375).astype(jnp.bfloat16)
    second_shift = bell_draw(streams_of[9], (D,), 0.5, 3.0, ((0, 32),))
    expand_weight = bell_draw(streams_of[10], (D, FF), D ** -0.5, 0.1875, ((0, 32),))
    expand_bias = bell_draw(streams_of[11], (FF,), 0.5, 3.0, ((0, 32),))
    contract_weight = bell_draw(streams_of[12], (FF, D), FF ** -0.5, 0.09375, ((0, 32),))
    contract_bias = bell_draw(streams_of[13], (D,), 0.5, 3.0, ((0, 32),))
    return dict(hidden_in=hidden_in, cotangent=cotangent, first_gain=first_gain, first_shift=first_shift, triple_weight=triple_weight, triple_bias=triple_bias, dense_weight=dense_weight, dense_bias=dense_bias, second_gain=second_gain, second_shift=second_shift, expand_weight=expand_weight, expand_bias=expand_bias, contract_weight=contract_weight, contract_bias=contract_bias)


top_precision = lax.Precision.HIGHEST
big_negative = -1e+30
epsilon = 1e-05

@jax.custom_vjp
def low(v):
    return lax.optimization_barrier(v.astype(jnp.bfloat16)).astype(jnp.float32)

@jax.custom_vjp
def low_back(v):
    return v

def low_keep(v):
    return (low(v), None)

def low_pass(kept, grad):
    return (grad,)

def back_keep(v):
    return (v, None)

def back_low(kept, grad):
    return (low(grad),)
low.defvjp(low_keep, low_pass)
low_back.defvjp(back_keep, back_low)

def layer_norm(values, gain, shift):
    average = lax.optimization_barrier(jnp.mean(values, axis=-1, keepdims=True))
    centered = values - average
    variance = lax.optimization_barrier(jnp.mean(centered * centered, axis=-1, keepdims=True))
    return centered * lax.rsqrt(variance + epsilon) * gain + shift

def rotary_tables(positions, rotary):
    half = rotary // 2
    frequency = 10000.0 ** (-(jnp.arange(half, dtype=jnp.float32) * 2.0 / rotary))
    angles = positions.astype(jnp.float32)[:, None] * frequency[None, :]
    angles = jnp.concatenate([angles, angles], axis=-1)
    return (jnp.cos(angles), jnp.sin(angles))

def rotate(values, cosine, sine):
    rotary = cosine.shape[-1]
    half = rotary // 2
    leading = values[..., :rotary]
    turned = jnp.concatenate([-leading[..., half:], leading[..., :half]], axis=-1)
    return jnp.concatenate([leading * cosine + turned * sine, values[..., rotary:]], axis=-1)

def attend(query, keys, values, block, scale):
    group, length, heads, depth = query.shape
    count = length // block

    def one_block(pieces):
        query_block, start = pieces
        scores = jnp.einsum('gbhe,glhe->ghbl', query_block, keys, precision=top_precision) * scale
        scores = low_back(scores)
        rows = start + lax.broadcasted_iota(jnp.int32, (block, length), 0)
        columns = lax.broadcasted_iota(jnp.int32, (block, length), 1)
        masked = jnp.where(columns <= rows, scores, big_negative)
        highest = lax.optimization_barrier(jnp.max(masked, axis=-1, keepdims=True))
        weights = jnp.exp(masked - highest)
        total = lax.optimization_barrier(jnp.sum(weights, axis=-1, keepdims=True))
        probability = low(weights / total)
        return jnp.einsum('ghbl,glhe->gbhe', probability, values, precision=top_precision)
    blocks = query.reshape(group, count, block, heads, depth).transpose(1, 0, 2, 3, 4)
    starts = jnp.arange(count, dtype=jnp.int32) * block
    outputs = lax.map(jax.checkpoint(one_block), (blocks, starts))
    return outputs.transpose(1, 0, 2, 3, 4).reshape(group, length, heads, depth)

def forward(params, source):
    first_gain, first_shift, triple_weight, triple_bias, dense_weight, dense_bias, second_gain, second_shift, expand_weight, expand_bias, contract_weight, contract_bias = params
    group, length, width = source.shape
    normed_one = low(layer_norm(source, first_gain, first_shift))
    normed_two = low(layer_norm(source, second_gain, second_shift))
    triple = jnp.einsum('gld,de->gle', normed_one, triple_weight, precision=top_precision) + triple_bias
    triple = low_back(triple).reshape(group, length, 3, H, HD)
    cosine, sine = rotary_tables(jnp.arange(length, dtype=jnp.int32), ROT)
    cosine = cosine[:, None, :]
    sine = sine[:, None, :]
    query = low_back(low(rotate(triple[:, :, 0], cosine, sine)))
    keys = low_back(low(rotate(triple[:, :, 1], cosine, sine)))
    values = low_back(low(triple[:, :, 2]))
    block = 512 if length % 512 == 0 else length
    context = attend(query, keys, values, block, 1.0 / math.sqrt(HD))
    context = low_back(low(context)).reshape(group, length, width)
    attended = jnp.einsum('gld,de->gle', context, dense_weight, precision=top_precision) + dense_bias
    expanded = low_back(jnp.einsum('gld,df->glf', normed_two, expand_weight, precision=top_precision) + expand_bias)
    activated = low(jax.nn.gelu(expanded, approximate=False))
    contracted = jnp.einsum('glf,fd->gld', activated, contract_weight, precision=top_precision) + contract_bias
    return source + attended + contracted

def reference(hidden_in, cotangent, first_gain, first_shift, triple_weight, triple_bias, dense_weight, dense_bias, second_gain, second_shift, expand_weight, expand_bias, contract_weight, contract_bias):
    params = tuple((item.astype(jnp.float32) for item in (first_gain, first_shift, triple_weight, triple_bias, dense_weight, dense_bias, second_gain, second_shift, expand_weight, expand_bias, contract_weight, contract_bias)))
    total_seqs, length, width = hidden_in.shape
    group = 2 if total_seqs % 2 == 0 else 1
    count = total_seqs // group
    sources = hidden_in.astype(jnp.float32).reshape(count, group, length, width)
    upstreams = cotangent.astype(jnp.float32).reshape(count, group, length, width)

    def one_group(carry, pieces):
        source, upstream = pieces
        output, pullback = jax.vjp(forward, params, source)
        grad_params, grad_source = pullback(upstream)
        carry = jax.tree.map(lambda left, right: left + right, carry, grad_params)
        return (carry, (output.astype(jnp.bfloat16), grad_source))
    zeros = jax.tree.map(jnp.zeros_like, params)
    totals, (outputs, grad_sources) = lax.scan(one_group, zeros, (sources, upstreams))
    return (outputs.reshape(total_seqs, length, width), grad_sources.reshape(total_seqs, length, width), totals[0], totals[1], totals[2], totals[3], totals[4], totals[5], totals[6], totals[7], totals[8], totals[9], totals[10], totals[11])
```

```python
import math

import jax
import jax.numpy as jnp
from jax import lax
from jax.experimental import pallas as pl
from jax.experimental.pallas import tpu as pltpu
from jax.sharding import PartitionSpec as P

H = 16
HD = 64
ROT = 16


big_negative = -1e30
epsilon = 1e-05


def layer_norm(values, gain, shift):
    average = jnp.mean(values, axis=-1, keepdims=True)
    centered = values - average
    variance = jnp.mean(centered * centered, axis=-1, keepdims=True)
    return centered * lax.rsqrt(variance + epsilon) * gain + shift


def rotary_tables(positions, width):
    half = ROT // 2
    entry = jnp.arange(HD, dtype=jnp.int32)
    index = (entry % half).astype(jnp.float32)
    frequency = 10000.0 ** (-(index * 2.0 / ROT))
    angles = positions.astype(jnp.float32)[:, None] * frequency[None, :]
    cosine, sine = jnp.cos(angles), jnp.sin(angles)
    keep = jnp.where(entry < ROT, cosine, 1.0)
    ahead = jnp.where(entry < half, -sine, 0.0)
    behind = jnp.where((entry >= half) & (entry < ROT), sine, 0.0)
    return tuple(jnp.tile(table, (1, width // HD)) for table in (keep, ahead, behind))


def shifted(values, amount):
    return jnp.concatenate([values[..., amount:], values[..., :amount]], axis=-1)


def rotate(values, tables, sign):
    keep, ahead, behind = tables
    half = ROT // 2
    return values * keep + sign * (
        shifted(values, half) * ahead + shifted(values, -half) * behind
    )


def attention_body(
    heads,
    block,
    q_ref,
    k_ref,
    v_ref,
    dc_ref,
    kt_ref,
    vt_ref,
    c_ref,
    dq_ref,
    dk_ref,
    dv_ref,
    s_ref,
    dk_acc,
    dv_acc,
):
    qi = pl.program_id(1)
    steps = pl.num_programs(1)
    scale = 1.0 / math.sqrt(HD)
    width = heads * HD

    @pl.when(qi == 0)
    def _():
        dk_acc[...] = jnp.zeros_like(dk_acc)
        dv_acc[...] = jnp.zeros_like(dv_acc)

    lane = lax.broadcasted_iota(jnp.int32, (block, width), 1) // HD
    causal = lax.broadcasted_iota(jnp.int32, (block, block), 0) <= lax.broadcasted_iota(
        jnp.int32, (block, block), 1
    )
    q_all = q_ref[...] * jnp.bfloat16(scale)
    dc_all = dc_ref[...]
    contexts = []
    grads = []
    nt = (((1,), (1,)), ((), ()))
    for h in range(heads):
        zero = jnp.zeros_like(q_all)
        q = jnp.where(lane == h, q_all, zero)
        dc = jnp.where(lane == h, dc_all, zero)
        rows = pl.ds(h * HD, HD)

        def scores(ki, q=q):
            keys = k_ref[pl.ds(ki * block, block), :]
            return lax.dot_general(keys, q, nt, preferred_element_type=jnp.float32)

        def first(ki, highest, scores=scores):
            s = scores(ki)
            s_ref[pl.ds(ki * block, block), :] = s
            return jnp.maximum(highest, jnp.max(s, axis=0, keepdims=True))

        diagonal = jnp.where(causal, scores(qi), big_negative)
        s_ref[pl.ds(qi * block, block), :] = diagonal
        highest = lax.fori_loop(0, qi, first, jnp.max(diagonal, axis=0, keepdims=True))

        def second(ki, carry, highest=highest, rows=rows):
            total, context = carry
            e = jnp.exp(s_ref[pl.ds(ki * block, block), :] - highest)
            total = total + jnp.sum(e, axis=0, keepdims=True)
            context = context + jnp.dot(
                vt_ref[rows, pl.ds(ki * block, block)],
                e.astype(jnp.bfloat16),
                preferred_element_type=jnp.float32,
            )
            return (total, context)

        total, context = lax.fori_loop(
            0,
            qi + 1,
            second,
            (jnp.zeros((1, block), jnp.float32), jnp.zeros((HD, block), jnp.float32)),
        )
        context = context / total
        log_total = highest + jnp.log(total)
        contexts.append(context)
        dct = dc_all[:, h * HD : (h + 1) * HD].astype(jnp.float32).T
        inner = jnp.sum(context * dct, axis=0, keepdims=True)

        def third(ki, grad, q=q, dc=dc, inner=inner, log_total=log_total, rows=rows):
            here = pl.ds(ki * block, block)
            p = jnp.exp(s_ref[here, :] - log_total)
            dp = lax.dot_general(v_ref[here, :], dc, nt, preferred_element_type=jnp.float32)
            ds = (p * (dp - inner)).astype(jnp.bfloat16)
            dv_acc[here, :] += jnp.dot(
                p.astype(jnp.bfloat16), dc, preferred_element_type=jnp.float32
            )
            dk_acc[here, :] += jnp.dot(ds, q, preferred_element_type=jnp.float32)
            return grad + jnp.dot(kt_ref[rows, here], ds, preferred_element_type=jnp.float32)

        grad = lax.fori_loop(0, qi + 1, third, jnp.zeros((HD, block), jnp.float32))
        grads.append(grad * scale)
    c_ref[...] = jnp.concatenate(contexts, axis=0).T.astype(jnp.bfloat16)
    dq_ref[...] = jnp.concatenate(grads, axis=0).T.astype(jnp.bfloat16)

    @pl.when(qi == steps - 1)
    def _():
        dk_ref[...] = dk_acc[...].astype(jnp.bfloat16)
        dv_ref[...] = dv_acc[...].astype(jnp.bfloat16)


def attention(parts):
    _, seqs, length, width = parts.shape
    heads = width // HD
    block = min(512, length)
    turned = parts[1:3].transpose(0, 1, 3, 2)

    def rows_of(which):
        return pl.BlockSpec((None, None, block, width), lambda s, i, w=which: (w, s, i, 0))

    def whole_of(which):
        return pl.BlockSpec((None, None, length, width), lambda s, i, w=which: (w, s, 0, 0))

    def turned_of(which):
        return pl.BlockSpec((None, None, width, length), lambda s, i, w=which: (w, s, 0, 0))

    out_rows = pl.BlockSpec((None, block, width), lambda s, i: (s, i, 0))
    out_whole = pl.BlockSpec((None, length, width), lambda s, i: (s, 0, 0))
    shape = jax.ShapeDtypeStruct((seqs, length, width), jnp.bfloat16)

    def body(*refs):
        attention_body(heads, block, *refs)

    return pl.pallas_call(
        body,
        grid=(seqs, length // block),
        in_specs=[rows_of(0), whole_of(1), whole_of(2), rows_of(3), turned_of(0), turned_of(1)],
        out_specs=[out_rows, out_rows, out_whole, out_whole],
        out_shape=[shape] * 4,
        scratch_shapes=[
            pltpu.VMEM((length, block), jnp.float32),
            pltpu.VMEM((length, width), jnp.float32),
            pltpu.VMEM((length, width), jnp.float32),
        ],
        compiler_params=pltpu.CompilerParams(
            dimension_semantics=("arbitrary", "arbitrary"), vmem_limit_bytes=50 * 1024 * 1024
        ),
        name="attention",
    )(parts, parts, parts, parts, turned, turned)


def scatter_sum(values, axes):
    return lax.psum_scatter(values, axes, scatter_dimension=0, tiled=True)


def local(
    hidden_in,
    cotangent,
    first_gain,
    first_shift,
    triple_weight,
    triple_bias,
    dense_weight,
    dense_bias,
    second_gain,
    second_shift,
    expand_weight,
    expand_bias,
    contract_weight,
    contract_bias,
):
    axes = ("dp", "seq")
    devices = lax.axis_size("dp") * lax.axis_size("seq")
    w_triple = lax.all_gather(triple_weight, axes, axis=0, tiled=True)
    vectors = (
        first_gain,
        first_shift,
        triple_bias,
        dense_bias,
        second_gain,
        second_shift,
        expand_bias,
        contract_bias,
    )
    stacked = lax.all_gather(jnp.concatenate(vectors), axes, axis=0, tiled=True)
    stacked = stacked.reshape(devices, -1)
    whole = []
    offset = 0
    for vector in vectors:
        size = vector.shape[0]
        whole.append(stacked[:, offset : offset + size].reshape(-1))
        offset += size
    gain_one, shift_one, b_triple, b_dense, gain_two, shift_two, b_expand, b_contract = whole
    w_dense = lax.all_gather(dense_weight, axes, axis=0, tiled=True)
    w_expand = lax.all_gather(expand_weight, axes, axis=0, tiled=True)
    w_contract = lax.all_gather(contract_weight, axes, axis=0, tiled=True)
    seqs, part_len, width = hidden_in.shape
    groups = lax.axis_size("seq")
    heads_here = H // groups
    tokens_here = seqs * part_len
    source = hidden_in.astype(jnp.float32).reshape(tokens_here, width)
    normed_one, pull_one = jax.vjp(
        layer_norm, source, gain_one.astype(jnp.float32), shift_one.astype(jnp.float32)
    )
    normed_two, pull_two = jax.vjp(
        layer_norm, source, gain_two.astype(jnp.float32), shift_two.astype(jnp.float32)
    )
    low_one = normed_one.astype(jnp.bfloat16)
    low_two = normed_two.astype(jnp.bfloat16)
    triple = jnp.dot(low_one, w_triple, preferred_element_type=jnp.float32) + b_triple.astype(
        jnp.float32
    )
    positions = lax.axis_index("seq") * part_len + jnp.arange(part_len, dtype=jnp.int32)
    tables = rotary_tables(positions, 2 * width)
    rotated = rotate(triple[:, : 2 * width].reshape(seqs, part_len, 2 * width), tables, 1.0)
    rotated = rotated.astype(jnp.bfloat16).reshape(tokens_here, 2 * width)
    upstream = cotangent.reshape(tokens_here, width)
    grad_context = jnp.einsum("td,ed->te", upstream, w_dense, preferred_element_type=jnp.float32)
    sending = jnp.stack(
        [
            rotated[:, :width],
            rotated[:, width:],
            triple[:, 2 * width :].astype(jnp.bfloat16),
            grad_context.astype(jnp.bfloat16),
        ]
    )
    mine = heads_here * HD
    sending = sending.reshape(4, seqs, part_len, groups, mine).transpose(3, 0, 1, 2, 4)
    received = lax.all_to_all(sending, "seq", split_axis=0, concat_axis=0, tiled=True)
    received = received.transpose(1, 2, 0, 3, 4).reshape(4, seqs, groups * part_len, mine)
    returned = jnp.stack(attention(received))
    returned = returned.reshape(4, seqs, groups, part_len, mine).transpose(2, 0, 1, 3, 4)
    returned = lax.all_to_all(returned, "seq", split_axis=0, concat_axis=0, tiled=True)
    returned = returned.transpose(1, 2, 3, 0, 4).reshape(4, tokens_here, width)
    context_flat = returned[0]
    attended = jnp.dot(context_flat, w_dense, preferred_element_type=jnp.float32) + b_dense.astype(
        jnp.float32
    )
    expanded = jnp.dot(low_two, w_expand, preferred_element_type=jnp.float32) + b_expand.astype(
        jnp.float32
    )
    activated, pull_gelu = jax.vjp(lambda inner: jax.nn.gelu(inner, approximate=False), expanded)
    low_act = activated.astype(jnp.bfloat16)
    contracted = jnp.dot(
        low_act, w_contract, preferred_element_type=jnp.float32
    ) + b_contract.astype(jnp.float32)
    block_out = (source + attended + contracted).astype(jnp.bfloat16).reshape(seqs, part_len, width)
    upstream_total = jnp.sum(upstream.astype(jnp.float32), axis=0)
    grad_w_dense = jnp.einsum(
        "td,te->de", context_flat, upstream, preferred_element_type=jnp.float32
    )
    grad_act = jnp.einsum(
        "td,fd->tf", upstream, w_contract, preferred_element_type=jnp.float32
    )
    grad_expanded = pull_gelu(grad_act)[0].astype(jnp.bfloat16)
    grad_w_contract = jnp.einsum("tf,td->fd", low_act, upstream, preferred_element_type=jnp.float32)
    grad_w_expand = jnp.einsum(
        "td,tf->df", low_two, grad_expanded, preferred_element_type=jnp.float32
    )
    grad_b_expand = jnp.sum(grad_expanded.astype(jnp.float32), axis=0)
    grad_second = jnp.einsum(
        "tf,df->td", grad_expanded, w_expand, preferred_element_type=jnp.float32
    )
    grad_source_two, grad_gain_two, grad_shift_two = pull_two(grad_second)
    grad_pair = jnp.concatenate([returned[1], returned[2]], axis=-1).astype(jnp.float32)
    grad_pair = rotate(grad_pair.reshape(seqs, part_len, 2 * width), tables, -1.0)
    grad_pair = grad_pair.astype(jnp.bfloat16).reshape(tokens_here, 2 * width)
    grad_triple = jnp.concatenate([grad_pair, returned[3]], axis=-1)
    grad_w_triple = jnp.einsum(
        "td,te->de", low_one, grad_triple, preferred_element_type=jnp.float32
    )
    grad_b_triple = jnp.sum(grad_triple.astype(jnp.float32), axis=0)
    grad_first = jnp.einsum(
        "te,de->td", grad_triple, w_triple, preferred_element_type=jnp.float32
    )
    grad_source_one, grad_gain_one, grad_shift_one = pull_one(grad_first)
    grad_input = (upstream.astype(jnp.float32) + grad_source_one + grad_source_two).reshape(
        seqs, part_len, width
    )
    totals = (
        grad_gain_one,
        grad_shift_one,
        grad_b_triple,
        upstream_total,
        grad_gain_two,
        grad_shift_two,
        grad_b_expand,
    )
    totals = [total.reshape(devices, -1) for total in totals]
    sizes = [total.shape[1] for total in totals]
    vector_grads = lax.psum_scatter(
        jnp.concatenate(totals, axis=1), axes, scatter_dimension=0, tiled=True
    ).reshape(-1)
    pieces = []
    offset = 0
    for size in sizes:
        pieces.append(vector_grads[offset : offset + size])
        offset += size
    out_gain_one, out_shift_one, out_b_triple, out_b_dense = pieces[:4]
    out_gain_two, out_shift_two, out_b_expand = pieces[4:]
    out_b_contract = out_b_dense
    out_w_contract = scatter_sum(grad_w_contract, axes)
    out_w_expand = scatter_sum(grad_w_expand, axes)
    out_w_dense = scatter_sum(grad_w_dense, axes)
    out_w_triple = scatter_sum(grad_w_triple, axes)
    return (
        block_out,
        grad_input,
        out_gain_one,
        out_shift_one,
        out_w_triple,
        out_b_triple,
        out_w_dense,
        out_b_dense,
        out_gain_two,
        out_shift_two,
        out_w_expand,
        out_b_expand,
        out_w_contract,
        out_b_contract,
    )


def solution(mesh):
    placed = (
        P("dp", "seq", None),
        P("dp", "seq", None),
        P(("dp", "seq")),
        P(("dp", "seq")),
        P(("dp", "seq"), None),
        P(("dp", "seq")),
        P(("dp", "seq"), None),
        P(("dp", "seq")),
        P(("dp", "seq")),
        P(("dp", "seq")),
        P(("dp", "seq"), None),
        P(("dp", "seq")),
        P(("dp", "seq"), None),
        P(("dp", "seq")),
    )
    return jax.shard_map(
        local,
        mesh=mesh,
        in_specs=placed,
        out_specs=(
            P("dp", "seq", None),
            P("dp", "seq", None),
            P(("dp", "seq")),
            P(("dp", "seq")),
            P(("dp", "seq"), None),
            P(("dp", "seq")),
            P(("dp", "seq"), None),
            P(("dp", "seq")),
            P(("dp", "seq")),
            P(("dp", "seq")),
            P(("dp", "seq"), None),
            P(("dp", "seq")),
            P(("dp", "seq"), None),
            P(("dp", "seq")),
        ),
        check_vma=False,
    )
```
